512 devices in a mesh: sec: 4 (over z_hi), dev: 128 (over z_lo, y, x, core).
Axes of the slice: x: 4, y: 4, z: 16 (z_hi: 4, z_lo: 4; z = z_hi * 4 + z_lo), core: 2. Of those that a mesh axis runs over, the one named last changes fastest.
Arguments:
- queries: bfloat16 [256, 8192], P('dev', 'sec'), may hold values from -24 to 24
- cache_keys: bfloat16 [256, 4, 512, 128], P('dev', 'sec'), may hold values from -24 to 24
- cache_values: bfloat16 [256, 4, 512, 128], P('dev', 'sec'), may hold values from -48 to 48
- lengths: int32 [256], P('dev'), may hold values from 2 to 512, as said below
- out_proj: bfloat16 [4096, 8192], P('dev', 'sec'), may hold values from -0.0625 to 0.0625
- residual: bfloat16 [256, 4096], P(None, 'dev'), may hold values from -3 to 3
- norm_gain: bfloat16 [4096], replicated, may hold values from 0.5 to 1.5
- expert_ids: int32 [256, 8], replicated, may hold values from 0 to 127, all different within a row; in each aligned block of 256 rows (0 to 255, 256 to 511, ...) at most 48 rows name the same one
- gate_weights: float32 [256, 8], replicated, may hold values from 0.5 to 1.5
- owners: int32 [128], replicated, may hold values from 0 to 127, each once
- gate_proj: bfloat16 [128, 768, 4096], P('dev', 'sec'), may hold values from -0.09375 to 0.09375
- up_proj: bfloat16 [128, 768, 4096], P('dev', 'sec'), may hold values from -0.09375 to 0.09375
- down_proj: bfloat16 [128, 768, 4096], P('dev', 'sec'), may hold values from -0.21875 to 0.21875
Outputs:
- output: bfloat16 [256, 4096], P(None, 'dev')
The draws below stay inside these ranges and needn't reach their ends.
Inputs may be any that keep to these rules, and one draw needn't show every extreme that they name: Row r's cache holds lengths[r] live positions from position 0; some row holds exactly 512. `expert_ids`: each row names 8 different experts; over all 256 rows no expert is named more than 48 times, a bound that some block reaches. Each index appears once; expert e's projections stand at index owners[e] of the expert projections.
All inputs are finite; a program needn't handle non-finite values.
Results may differ from the reference program's by a relative error of at most 0.009.
Values may be sent and summed in bfloat16 or wider, within the bound.
No kernel may reach another device: no remote copies, remote signals or barrier semaphores. Data moves between devices by JAX's collectives and lax.ppermute only.
A program may use at most 64 MiB of HBM per device.

```python
import math
import jax
import jax.numpy as jnp
import numpy as np
from jax import lax

D = 4096
HEADS = 64
KV_HEADS = 4
HEAD_DIM = 128
TOPK = 8
FF_WIN = 768
CACHE = 512
EXPERTS = 128
ROWS = 256
CAP = 48


def draw_queries(key, part):
    baseline = jnp.clip(jax.random.normal(jax.random.fold_in(key, 11), (ROWS, HEADS * HEAD_DIM), jnp.float32), -6.0, 6.0)
    return baseline.astype(jnp.bfloat16)


def draw_cache_keys(key, part):
    baseline = jnp.clip(jax.random.normal(jax.random.fold_in(key, 23), (ROWS, KV_HEADS, CACHE, HEAD_DIM), jnp.float32), -6.0, 6.0)
    return baseline.astype(jnp.bfloat16)


def draw_lengths(key, part):
    subkeys = jax.random.split(jax.random.fold_in(key, 31), 3)
    lengths_out = jax.random.randint(subkeys[0], (ROWS,), 2, CACHE + 1, dtype=jnp.int32)
    longest = jax.random.randint(subkeys[1], (), 0, ROWS, dtype=jnp.int32)
    offset = jax.random.randint(subkeys[2], (), 1, ROWS, dtype=jnp.int32)
    shortest = (longest + offset) % ROWS
    return lengths_out.at[longest].set(CACHE).at[shortest].set(2)


def block_scale(key, extent, cuts, low, largest):
    factor_of, own = 1.0, jax.random.fold_in(key, 6)
    for dim, shards_of in cuts:
        draws = jnp.exp(jax.random.uniform(jax.random.fold_in(own, dim), (shards_of,), jnp.float32, low / len(cuts), largest / len(cuts)))
        factor_of = factor_of * jnp.repeat(draws, extent[dim] // shards_of).reshape([-1 if axis == dim else 1 for axis in range(len(extent))])
    return factor_of


def routed_block(rng, own, number, rows, amount, top, most, slope):
    ranking = jax.random.permutation(rng, amount)
    crowded, usual = shares(amount, rows * top, most, slope, True), shares(amount, rows * top, most, slope, False)
    places = jnp.arange(amount)

    def named(sizes, rotation):
        used = int((sizes > 0).sum())
        fixed = max(1, used // 4)
        shifted = fixed + (places - fixed + rotation * (used - fixed)) % max(1, amount - fixed)
        return jnp.zeros((amount,), jnp.int32).at[ranking[jnp.where(places < fixed, places, shifted)]].set(jnp.asarray(sizes, jnp.int32))

    sizes = jnp.where(number % 4 == 0, named(crowded, number // 4), named(usual, number - number // 4 - 1))
    mixed = jax.random.permutation(jax.random.fold_in(own, 3), amount)
    giver, taker = mixed[0:amount // 2 * 2:2], mixed[1:amount // 2 * 2:2]
    slack = jnp.minimum(sizes[giver] - 1, most - sizes[taker]) // 2
    slack = jnp.where((giver == ranking[0]) | (taker == ranking[0]) | (sizes[taker] == 0), 0, jnp.maximum(slack, 0))
    shifted = jax.random.randint(jax.random.fold_in(own, 4), (amount // 2,), 0, 1 << 20) % (slack + 1)
    sizes = sizes.at[giver].add(-shifted).at[taker].add(shifted)
    items = jnp.searchsorted(jnp.cumsum(sizes), jnp.arange(rows * top), side="right").astype(jnp.int32)
    grid = items.reshape(top, rows).T
    grid = grid[jax.random.permutation(jax.random.fold_in(own, 1), rows)]
    rotation = jax.random.randint(jax.random.fold_in(own, 2), (rows, 1), 0, top)
    return jnp.take_along_axis(grid, (jnp.arange(top)[None, :] + rotation) % top, axis=1)


def shares(count, total, bound, skew, full):
    loads = [(1 << 20) // math.isqrt(standing ** skew) + 1 for standing in range(1, count + 1)]
    largest = bound if full else min(bound, max(-(-total // count), total * loads[0] // sum(loads)))
    least = 1 if total - largest >= count - 1 else 0
    holding, rest = [largest] + [least] * (count - 1), total - largest - least * (count - 1)
    while rest > 0:
        movable = [i for i in range(1, count) if holding[i] < largest] or [i for i in range(1, count) if holding[i] < bound]
        pool, budget = sum([loads[i] for i in movable]), rest
        for i in movable:
            more = min(bound - holding[i], max(1, budget * loads[i] // pool), rest)
            holding[i] = holding[i] + more
            rest = rest - more
    return np.array(holding)


def gaussian(key, shape, deviation, bound, cuts=(), kind=jnp.bfloat16):
    array = deviation * jax.random.normal(key, shape, jnp.float32)
    if cuts:
        array = array * block_scale(key, shape, cuts, -0.22, 0.18)
    return jnp.clip(array, -bound, bound).astype(kind)


def setup_inputs(seed: int = 0) -> dict:
    keys = jax.random.split(jax.random.key(seed), 14)
    queries = draw_queries(jax.random.fold_in(keys[13], 71), 0)
    cache_keys = draw_cache_keys(jax.random.fold_in(keys[13], 71), 0)
    cache_values = gaussian(keys[2], (ROWS, KV_HEADS, CACHE, HEAD_DIM), 8.0, 48.0, ((0, 128), (1, 4)))
    lengths = draw_lengths(jax.random.fold_in(keys[13], 71), 0)
    out_proj = gaussian(keys[4], (D, HEADS * HEAD_DIM), (HEADS * HEAD_DIM) ** -0.5, 0.0625, ((0, 128), (1, 4)))
    residual = gaussian(keys[5], (ROWS, D), 0.5, 3.0, ((1, 128),))
    norm_gain = jnp.clip(1.0 + 0.1 * jax.random.normal(keys[6], (D,), jnp.float32), 0.5, 1.5).astype(jnp.bfloat16)
    expert_ids_keys = jax.random.split(jax.random.fold_in(keys[7], 1), ROWS // ROWS)
    expert_ids_turns = jax.random.permutation(jax.random.fold_in(keys[7], 3), ROWS // ROWS)
    expert_ids = jax.vmap(lambda own, number: routed_block(jax.random.fold_in(keys[7], 2), own, number, ROWS, EXPERTS, TOPK, CAP, 2))(expert_ids_keys, expert_ids_turns).reshape((ROWS, TOPK))
    gate_weights = jnp.clip(jax.random.uniform(keys[8], (ROWS, TOPK), jnp.float32, 0.5, 1.5), 0.5, 1.5)
    owners = jax.random.permutation(keys[9], EXPERTS).astype(jnp.int32)
    gate_proj = gaussian(keys[10], (EXPERTS, FF_WIN, D), D ** -0.5, 0.09375, ((0, 128), (1, 4)))
    up_proj = gaussian(keys[11], (EXPERTS, FF_WIN, D), D ** -0.5, 0.09375, ((0, 128), (1, 4)))
    down_proj = gaussian(keys[12], (EXPERTS, FF_WIN, D), FF_WIN ** -0.5, 0.21875, ((0, 128), (1, 4)))
    return dict(queries=queries, cache_keys=cache_keys, cache_values=cache_values, lengths=lengths, out_proj=out_proj, residual=residual, norm_gain=norm_gain, expert_ids=expert_ids, gate_weights=gate_weights, owners=owners, gate_proj=gate_proj, up_proj=up_proj, down_proj=down_proj)


epsilon = 1e-05

def slot_targets(expert_ids, owners, capacity):
    experts = owners.shape[0]
    flat_ids = expert_ids.reshape(-1)
    one_hot = (flat_ids[:, None] == jnp.arange(experts, dtype=jnp.int32)[None, :]).astype(jnp.int32)
    before = jnp.cumsum(one_hot, axis=0) - one_hot
    position = lax.optimization_barrier(jnp.sum(before * one_hot, axis=1))
    holder = lax.optimization_barrier(jnp.sum(one_hot * owners[None, :], axis=1))
    return (holder * capacity + position).reshape(expert_ids.shape)

def routing_tables(expert_ids, gate_weights, owners, capacity):
    target = slot_targets(expert_ids, owners, capacity)
    places = jnp.arange(owners.shape[0] * capacity, dtype=jnp.int32)
    matched = target[None, :, :] == places[:, None, None]
    sending = jnp.any(matched, axis=2)
    weighting = lax.optimization_barrier(jnp.sum(jnp.where(matched, gate_weights[None, :, :], jnp.zeros_like(gate_weights)[None, :, :]), axis=2))
    return (sending, weighting)

def times_transpose(left, right):
    return lax.dot_general(left, right, (((1,), (1,)), ((), ())), preferred_element_type=jnp.float32)

def attend(queries, cache_keys, cache_values, lengths):
    rows, kv_heads, key_span, head_dim = cache_keys.shape
    group_size = queries.shape[1] // (kv_heads * head_dim)
    grouped = queries.reshape(rows, kv_heads, group_size, head_dim)
    scores = jnp.einsum('rkgd,rktd->rkgt', grouped.astype(jnp.float32), cache_keys.astype(jnp.float32)) / math.sqrt(head_dim)
    live_mask = jnp.arange(key_span, dtype=jnp.int32)[None, None, None, :] < lengths[:, None, None, None]
    scores = jnp.where(live_mask, scores, -jnp.inf)
    row_top = lax.optimization_barrier(jnp.max(scores, axis=-1, keepdims=True))
    raised = jnp.exp(scores - row_top)
    soft_weight = (raised / lax.optimization_barrier(jnp.sum(raised, axis=-1, keepdims=True))).astype(jnp.bfloat16)
    head_out = jnp.einsum('rkgt,rktd->rkgd', soft_weight.astype(jnp.float32), cache_values.astype(jnp.float32))
    return head_out.astype(jnp.bfloat16).reshape(rows, -1)

def root_norm(arrived, norm_gain):
    square_mean = lax.optimization_barrier(jnp.mean(arrived * arrived, axis=-1, keepdims=True))
    return (arrived * lax.rsqrt(square_mean + epsilon) * norm_gain.astype(arrived.dtype)).astype(jnp.bfloat16)

def expert_ffn(normed, gate_w, up_w, down_w):
    gate_act = times_transpose(normed, gate_w)
    up_act = times_transpose(normed, up_w)
    hidden = (jax.nn.silu(gate_act) * up_act).astype(jnp.bfloat16)
    return jnp.dot(hidden, down_w, preferred_element_type=jnp.float32)

def expert_packed(packed):
    return expert_ffn(packed[0], packed[1], packed[2], packed[3])

def reference(queries, cache_keys, cache_values, lengths, out_proj, residual, norm_gain, expert_ids, gate_weights, owners, gate_proj, up_proj, down_proj):
    head_out = attend(queries, cache_keys, cache_values, lengths)
    attention_out = times_transpose(head_out, out_proj)
    hidden_in = (residual.astype(jnp.float32) + attention_out).astype(jnp.bfloat16)
    sending, weighting = routing_tables(expert_ids, gate_weights, owners, CAP)
    arrived = jnp.dot(sending.astype(jnp.bfloat16), hidden_in, preferred_element_type=jnp.float32)
    normed = root_norm(arrived, norm_gain).reshape(EXPERTS, CAP, D)
    expert_out = lax.map(expert_packed, (normed, gate_proj, up_proj, down_proj)).reshape(EXPERTS * CAP, D)
    place_weight = lax.optimization_barrier(jnp.sum(weighting, axis=1))
    weighted = (expert_out * place_weight[:, None]).astype(jnp.bfloat16)
    moe = jnp.dot(sending.T.astype(jnp.bfloat16), weighted, preferred_element_type=jnp.float32)
    return (residual.astype(jnp.float32) + attention_out + moe).astype(jnp.bfloat16)
```

```python
import math

import jax
import jax.numpy as jnp
from jax import lax
from jax.experimental import pallas as pl
from jax.experimental.pallas import tpu as pltpu
from jax.sharding import PartitionSpec as P

epsilon = 1e-05

BANDS = 4
PART = 12
ROW = 16


def attend(queries, cache_keys, cache_values, lengths):
    rows, kv_heads, key_span, head_dim = cache_keys.shape
    group_size = queries.shape[1] // (kv_heads * head_dim)
    grouped = queries.reshape(rows, kv_heads, group_size, head_dim)
    scores = jnp.einsum(
        "rkgd,rktd->rkgt", grouped, cache_keys, preferred_element_type=jnp.float32
    ) / math.sqrt(head_dim)
    live_mask = (
        jnp.arange(key_span, dtype=jnp.int32)[None, None, None, :] < lengths[:, None, None, None]
    )
    scores = jnp.where(live_mask, scores, -jnp.inf)
    row_top = jnp.max(scores, axis=-1, keepdims=True)
    raised = jnp.exp(scores - row_top)
    soft_weight = (raised / jnp.sum(raised, axis=-1, keepdims=True)).astype(jnp.bfloat16)
    head_out = jnp.einsum(
        "rkgt,rktd->rkgd", soft_weight, cache_values, preferred_element_type=jnp.float32
    )
    return head_out.astype(jnp.bfloat16).reshape(rows, -1)


def nt_dot(left, right):
    return lax.dot_general(
        left, right, (((1,), (1,)), ((), ())), preferred_element_type=jnp.float32
    )


def iota(shape, dim):
    return lax.broadcasted_iota(jnp.int32, shape, dim)


def one_hot(condition):
    return jnp.where(condition, 1.0, 0.0).astype(jnp.bfloat16)


def routing_kernel(me_ref, ids_ref, gates_ref, owners_ref, table_ref, weight_ref, swap_ref, slot_ref):
    top_count, rows = ids_ref.shape
    experts = owners_ref.shape[1]
    me = me_ref[0]
    ids = ids_ref[...]
    owners = owners_ref[...]
    named = jnp.zeros((experts, rows), jnp.float32)
    expert_at = iota((experts, rows), 0)
    for k in range(top_count):
        named = jnp.where(ids[k : k + 1, :] == expert_at, 1.0, named)
    holds = one_hot(owners == iota((experts, experts), 0))
    routed = jnp.dot(holds, named.astype(jnp.bfloat16), preferred_element_type=jnp.float32)
    earlier = one_hot(iota((rows, rows), 0) < iota((rows, rows), 1))
    before = jnp.dot(routed.astype(jnp.bfloat16), earlier, preferred_element_type=jnp.float32)
    slots = jnp.where(routed > 0.5, before, -1.0)
    slot_ref[...] = slots

    mine = jnp.sum(
        jnp.where(owners == me, iota(owners.shape, 1), 0), axis=1, keepdims=True
    )
    row_gate = jnp.sum(jnp.where(ids == mine, gates_ref[...], 0.0), axis=0, keepdims=True)
    row_slot = jnp.sum(jnp.where(iota(slots.shape, 0) == me, slots, 0.0), axis=0, keepdims=True)
    at = iota((BANDS * ROW, rows), 0)
    place = jnp.where(at % ROW < PART, at // ROW * PART + at % ROW, rows + 1).astype(jnp.float32)
    weight_ref[...] = jnp.sum(jnp.where(row_slot == place, row_gate, 0.0), axis=1, keepdims=True)

    lanes = swap_ref.shape[0]
    source = iota((lanes, lanes), 0)
    target = iota((lanes, lanes), 1)
    swapped = target % 32 + target // 128 * 32 + target // 32 % 4 * 128
    swap_ref[...] = one_hot(source == swapped)

    row_at = iota((ROW, rows), 0)
    row_place = jnp.where(row_at < PART, row_at, 4 * rows).astype(jnp.float32)

    def fill(expert, carry):
        slot = slot_ref[pl.ds(expert, 1), :]
        for band in range(BANDS):
            table_ref[expert, :, band * rows : (band + 1) * rows] = one_hot(
                slot - float(band * PART) == row_place
            )
        return carry

    lax.fori_loop(0, experts, fill, 0, unroll=4)


def routing(expert_ids, gate_weights, owners, me):
    rows, top_count = expert_ids.shape
    experts = owners.shape[0]
    vmem = pl.BlockSpec(memory_space=pltpu.VMEM)
    return pl.pallas_call(
        routing_kernel,
        out_shape=(
            jax.ShapeDtypeStruct((experts, ROW, BANDS * rows), jnp.bfloat16),
            jax.ShapeDtypeStruct((BANDS * ROW, 1), jnp.float32),
            jax.ShapeDtypeStruct((512, 512), jnp.bfloat16),
        ),
        in_specs=[pl.BlockSpec(memory_space=pltpu.SMEM), vmem, vmem, vmem],
        out_specs=(vmem, vmem, vmem),
        scratch_shapes=[pltpu.VMEM((experts, rows), jnp.float32)],
        name="routing",
    )(me.reshape(1), expert_ids.T, gate_weights.T, owners.reshape(1, -1))


def dispatch_kernel(parts_ref, residual_ref, table_ref, send_ref, base_ref, wide_ref):
    groups, cols, rows = parts_ref.shape
    source = iota((rows, rows), 0)
    target = iota((rows, rows), 1)
    half = rows // 2
    order = one_hot(source == target // 2 % 2 * half + target // 4 * 2 + target % 2)
    parts = jnp.dot(
        parts_ref[...].reshape(groups * cols, rows), order, preferred_element_type=jnp.float32
    )
    attention = parts[:cols]
    for group in range(1, groups):
        attention = attention + parts[group * cols : (group + 1) * cols]
    base = residual_ref[...].astype(jnp.float32) + attention
    base_ref[...] = base
    hidden_in = base.astype(jnp.bfloat16)
    wide_ref[...] = jnp.zeros(wide_ref.shape, jnp.bfloat16)
    for band in range(BANDS):
        wide_ref[band * cols : (band + 1) * cols, band * rows : (band + 1) * rows] = hidden_in
    experts = table_ref.shape[0]
    table = table_ref[...].reshape(experts * ROW, BANDS * rows)
    sent = nt_dot(table, wide_ref[...]).astype(jnp.bfloat16)
    send_ref[...] = sent.reshape(experts, ROW, BANDS * cols)[:, :PART, :]


def dispatch(parts, residual, table):
    groups, cols, rows = parts.shape
    experts = table.shape[0]
    vmem = pl.BlockSpec(memory_space=pltpu.VMEM)
    return pl.pallas_call(
        dispatch_kernel,
        out_shape=(
            jax.ShapeDtypeStruct((experts, PART, BANDS * cols), jnp.bfloat16),
            jax.ShapeDtypeStruct((cols, rows), jnp.float32),
        ),
        in_specs=[vmem] * 3,
        out_specs=(vmem, vmem),
        scratch_shapes=[pltpu.VMEM((BANDS * cols, BANDS * rows), jnp.bfloat16)],
        name="dispatch",
    )(parts, residual, table)


def expert_kernel(
    inbound_ref, gain_ref, weight_ref, swap_ref, gate_ref, up_ref, down_ref, send_ref, fold_ref, flat_ref
):
    devices = inbound_ref.shape[0]
    width = gain_ref.shape[1]
    tiles = devices // BANDS
    fold_ref[...] = jnp.zeros(fold_ref.shape, fold_ref.dtype)
    for device in range(devices):
        tile, lane = device // BANDS, device % BANDS
        fold_ref[tile * ROW : tile * ROW + PART, lane * 128 : (lane + 1) * 128] = inbound_ref[device]
    swap = swap_ref[...]
    turned = jnp.dot(fold_ref[...], swap, preferred_element_type=jnp.float32)
    for tile in range(tiles):
        for band in range(BANDS):
            flat_ref[band * ROW : (band + 1) * ROW, tile * 128 : (tile + 1) * 128] = turned[
                tile * ROW : (tile + 1) * ROW, band * 128 : (band + 1) * 128
            ]
    arrived = flat_ref[...]
    square_mean = jnp.sum(arrived * arrived, axis=1, keepdims=True) / width
    normed = (
        arrived * lax.rsqrt(square_mean + epsilon) * gain_ref[...].astype(jnp.float32)
    ).astype(jnp.bfloat16)
    gate_act = nt_dot(normed, gate_ref[...])
    up_act = nt_dot(normed, up_ref[...])
    hidden = (jax.nn.silu(gate_act) * up_act).astype(jnp.bfloat16)
    expert_out = jnp.dot(hidden, down_ref[...], preferred_element_type=jnp.float32)
    weighted = (expert_out * weight_ref[...]).astype(jnp.bfloat16)
    for tile in range(tiles):
        for band in range(BANDS):
            fold_ref[tile * ROW : (tile + 1) * ROW, band * 128 : (band + 1) * 128] = weighted[
                band * ROW : (band + 1) * ROW, tile * 128 : (tile + 1) * 128
            ]
    back = jnp.dot(fold_ref[...], swap, preferred_element_type=jnp.float32).astype(jnp.bfloat16)
    for device in range(devices):
        tile, lane = device // BANDS, device % BANDS
        send_ref[device] = back[tile * ROW : tile * ROW + PART, lane * 128 : (lane + 1) * 128]


def expert_layer(inbound, norm_gain, weight, swap, gate_proj, up_proj, down_proj):
    devices = inbound.shape[0]
    width = norm_gain.shape[0]
    vmem = pl.BlockSpec(memory_space=pltpu.VMEM)
    return pl.pallas_call(
        expert_kernel,
        out_shape=jax.ShapeDtypeStruct(inbound.shape, jnp.bfloat16),
        in_specs=[vmem] * 7,
        out_specs=vmem,
        scratch_shapes=[
            pltpu.VMEM((devices // BANDS * ROW, 512), jnp.bfloat16),
            pltpu.VMEM((BANDS * ROW, width), jnp.float32),
        ],
        name="expert_layer",
    )(inbound, norm_gain.reshape(1, -1), weight, swap, gate_proj, up_proj, down_proj)


def combine_kernel(returned_ref, table_ref, parts_ref, rows_ref):
    experts = returned_ref.shape[0]
    cols, rows = parts_ref.shape[1:]
    rows_ref[...] = jnp.zeros(rows_ref.shape, rows_ref.dtype)
    for expert in range(experts):
        rows_ref[expert * ROW : expert * ROW + PART, :] = returned_ref[expert]
    table = table_ref[...].reshape(experts * ROW, BANDS * rows)
    mixed = lax.dot_general(
        rows_ref[...], table, (((0,), (0,)), ((), ())), preferred_element_type=jnp.float32
    )
    moe = mixed[:cols, :rows]
    for band in range(1, BANDS):
        moe = moe + mixed[band * cols : (band + 1) * cols, band * rows : (band + 1) * rows]
    moe = moe.astype(jnp.bfloat16)
    for group in range(parts_ref.shape[0]):
        parts_ref[group] = moe


def combine(returned, table, groups, cols, rows):
    experts = returned.shape[0]
    vmem = pl.BlockSpec(memory_space=pltpu.VMEM)
    return pl.pallas_call(
        combine_kernel,
        out_shape=jax.ShapeDtypeStruct((groups, cols, rows), jnp.bfloat16),
        in_specs=[vmem] * 2,
        out_specs=vmem,
        scratch_shapes=[pltpu.VMEM((experts * ROW, BANDS * cols), jnp.bfloat16)],
        name="combine",
    )(returned, table)


def shards(
    queries,
    cache_keys,
    cache_values,
    lengths,
    out_proj,
    residual,
    norm_gain,
    expert_ids,
    gate_weights,
    owners,
    gate_proj,
    up_proj,
    down_proj,
):
    rows, cols = residual.shape
    groups = lax.axis_size("sec")
    devices = lax.axis_size("dev")
    chips = devices // 2
    me = lax.axis_index("dev")
    table, weight, swap = routing(expert_ids, gate_weights, owners, me)

    head_out = attend(queries, cache_keys, cache_values, lengths)
    same_core = [[2 * chip + core for chip in range(chips)] for core in range(2)]
    swap_core = [(device, device ^ 1) for device in range(devices)]
    gathered = lax.all_to_all(
        jnp.broadcast_to(head_out[None], (chips,) + head_out.shape),
        "dev",
        0,
        0,
        tiled=True,
        axis_index_groups=same_core,
    )
    gathered = gathered.reshape(-1, head_out.shape[1])
    other = lax.ppermute(gathered, "dev", swap_core)
    own_part = nt_dot(out_proj, gathered).astype(jnp.bfloat16)
    other_part = nt_dot(out_proj, other).astype(jnp.bfloat16)
    first = me % 2 == 0
    part = jnp.concatenate(
        [jnp.where(first, own_part, other_part), jnp.where(first, other_part, own_part)], axis=1
    )
    parts = lax.all_to_all(
        jnp.broadcast_to(part[None], (groups,) + part.shape), "sec", 0, 0, tiled=True
    )
    outbound, base = dispatch(parts, residual.T, table)
    inbound = lax.all_to_all(outbound, "dev", 0, 0, tiled=True)
    weighted = expert_layer(
        inbound, norm_gain, weight, swap, gate_proj[0], up_proj[0], down_proj[0]
    )
    returned = lax.all_to_all(weighted, "dev", 0, 0, tiled=True)
    moe_parts = lax.all_to_all(
        combine(returned, table, groups, cols, rows), "sec", 0, 0, tiled=True
    )
    moe = jnp.sum(moe_parts.astype(jnp.float32), axis=0)
    return (base + moe).astype(jnp.bfloat16).T


def solution(mesh):
    in_specs = (
        P("dev", "sec"),
        P("dev", "sec", None, None),
        P("dev", "sec", None, None),
        P("dev"),
        P("dev", "sec"),
        P(None, "dev"),
        P(),
        P(),
        P(),
        P(),
        P("dev", "sec", None),
        P("dev", "sec", None),
        P("dev", "sec", None),
    )
    out_specs = P(None, "dev")
    return jax.shard_map(shards, mesh=mesh, in_specs=in_specs, out_specs=out_specs, check_vma=False)
```

```python
import math

import jax
import jax.numpy as jnp
from jax import lax
from jax.experimental import pallas as pl
from jax.experimental.pallas import tpu as pltpu
from jax.sharding import PartitionSpec as P

epsilon = 1e-05

PLANES = 4
PLANE = 32
CAP = 48


def attend(queries, cache_keys, cache_values, lengths):
    rows, kv_heads, key_span, head_dim = cache_keys.shape
    group_size = queries.shape[1] // (kv_heads * head_dim)
    grouped = queries.reshape(rows, kv_heads, group_size, head_dim)
    scores = jnp.einsum(
        "rkgd,rktd->rkgt", grouped, cache_keys, preferred_element_type=jnp.float32
    ) / math.sqrt(head_dim)
    live_mask = (
        jnp.arange(key_span, dtype=jnp.int32)[None, None, None, :] < lengths[:, None, None, None]
    )
    scores = jnp.where(live_mask, scores, -jnp.inf)
    row_top = jnp.max(scores, axis=-1, keepdims=True)
    raised = jnp.exp(scores - row_top)
    soft_weight = (raised / jnp.sum(raised, axis=-1, keepdims=True)).astype(jnp.bfloat16)
    head_out = jnp.einsum(
        "rkgt,rktd->rkgd", soft_weight, cache_values, preferred_element_type=jnp.float32
    )
    return head_out.astype(jnp.bfloat16).reshape(rows, -1)


def nt_dot(left, right):
    return lax.dot_general(
        left, right, (((1,), (1,)), ((), ())), preferred_element_type=jnp.float32
    )


def iota(shape, dim):
    return lax.broadcasted_iota(jnp.int32, shape, dim)


def one_hot(condition):
    return jnp.where(condition, 1.0, 0.0).astype(jnp.bfloat16)


def routing_kernel(me_ref, ids_ref, gates_ref, owners_ref, table_ref, weight_ref, swap_ref, slot_ref):
    top_count, rows = ids_ref.shape
    experts = owners_ref.shape[1]
    me = me_ref[0]
    ids = ids_ref[...]
    owners = owners_ref[...]
    named = jnp.zeros((experts, rows), jnp.float32)
    expert_at = iota((experts, rows), 0)
    for k in range(top_count):
        named = jnp.where(ids[k : k + 1, :] == expert_at, 1.0, named)
    holds = one_hot(owners == iota((PLANE, experts), 0) + me // PLANE * PLANE)
    routed = jnp.dot(holds, named.astype(jnp.bfloat16), preferred_element_type=jnp.float32)
    earlier = one_hot(iota((rows, rows), 0) < iota((rows, rows), 1))
    before = jnp.dot(routed.astype(jnp.bfloat16), earlier, preferred_element_type=jnp.float32)
    slots = jnp.where(routed > 0.5, before, -1.0)
    slot_ref[...] = slots

    mine = jnp.sum(
        jnp.where(owners == me, iota(owners.shape, 1), 0), axis=1, keepdims=True
    )
    row_gate = jnp.sum(jnp.where(ids == mine, gates_ref[...], 0.0), axis=0, keepdims=True)
    row_slot = jnp.sum(
        jnp.where(iota(slots.shape, 0) == me % PLANE, slots, 0.0), axis=0, keepdims=True
    )
    place = iota((CAP, rows), 0).astype(jnp.float32)
    weight_ref[...] = jnp.sum(jnp.where(row_slot == place, row_gate, 0.0), axis=1, keepdims=True)

    lanes = swap_ref.shape[0]
    source = iota((lanes, lanes), 0)
    target = iota((lanes, lanes), 1)
    swapped = target % 32 + target // 128 * 32 + target // 32 % 4 * 128
    swap_ref[...] = one_hot(source == swapped)

    for holder in range(PLANE):
        table_ref[holder * CAP : (holder + 1) * CAP, :] = one_hot(
            slot_ref[holder : holder + 1, :] == place
        )


def routing(expert_ids, gate_weights, owners, me):
    rows, top_count = expert_ids.shape
    vmem = pl.BlockSpec(memory_space=pltpu.VMEM)
    return pl.pallas_call(
        routing_kernel,
        out_shape=(
            jax.ShapeDtypeStruct((PLANE * CAP, rows), jnp.bfloat16),
            jax.ShapeDtypeStruct((CAP, 1), jnp.float32),
            jax.ShapeDtypeStruct((512, 512), jnp.bfloat16),
        ),
        in_specs=[pl.BlockSpec(memory_space=pltpu.SMEM), vmem, vmem, vmem],
        out_specs=(vmem, vmem, vmem),
        scratch_shapes=[pltpu.VMEM((PLANE, rows), jnp.float32)],
        name="routing",
    )(me.reshape(1), expert_ids.T, gate_weights.T, owners.reshape(1, -1))


def dispatch_kernel(me_ref, parts_ref, table_ref, send_ref, base_ref, wide_ref):
    column, cols, rows = parts_ref.shape
    groups = column // PLANES
    own = base_ref.shape[0]
    share = own // groups
    source = iota((rows, rows), 0)
    target = iota((rows, rows), 1)
    half = rows // 2
    order = one_hot(source == target // 2 % 2 * half + target // 4 * 2 + target % 2)
    for plane in range(PLANES):
        stacked = jnp.concatenate(
            [parts_ref[group * PLANES + plane, :own, :] for group in range(groups)], axis=0
        )
        parts = jnp.dot(stacked, order, preferred_element_type=jnp.float32)
        base = jnp.concatenate(
            [parts_ref[group * PLANES + plane, own:, :] for group in range(groups)], axis=0
        ).astype(jnp.float32)
        for group in range(groups):
            base = base + parts[group * own : (group + 1) * own]
        wide_ref[plane * own : (plane + 1) * own, :] = base
    base_ref[...] = wide_ref[pl.ds(pl.multiple_of(me_ref[0] // PLANE * own, own), own), :]
    hidden_in = wide_ref[...].astype(jnp.bfloat16)
    sent = nt_dot(table_ref[...], hidden_in).astype(jnp.bfloat16)
    send_ref[...] = sent.reshape(send_ref.shape)


def dispatch(parts, table, me, own):
    rows = parts.shape[2]
    vmem = pl.BlockSpec(memory_space=pltpu.VMEM)
    return pl.pallas_call(
        dispatch_kernel,
        out_shape=(
            jax.ShapeDtypeStruct((PLANE, CAP, PLANES * own), jnp.bfloat16),
            jax.ShapeDtypeStruct((own, rows), jnp.float32),
        ),
        in_specs=[pl.BlockSpec(memory_space=pltpu.SMEM), vmem, vmem],
        out_specs=(vmem, vmem),
        scratch_shapes=[pltpu.VMEM((PLANES * own, rows), jnp.float32)],
        name="dispatch",
    )(me.reshape(1), parts, table)


def expert_kernel(
    inbound_ref, gain_ref, weight_ref, swap_ref, gate_ref, up_ref, down_ref, send_ref, fold_ref, flat_ref
):
    width = gain_ref.shape[1]
    span = width // PLANES
    tiles = PLANE // 4
    for block in range(PLANE):
        tile, lane = block // 4, block % 4
        fold_ref[tile * CAP : (tile + 1) * CAP, lane * 128 : (lane + 1) * 128] = inbound_ref[block]
    swap = swap_ref[...]
    turned = jnp.dot(fold_ref[...], swap, preferred_element_type=jnp.float32)
    for tile in range(tiles):
        for plane in range(PLANES):
            at = plane * span + tile * 128
            flat_ref[:, at : at + 128] = turned[
                tile * CAP : (tile + 1) * CAP, plane * 128 : (plane + 1) * 128
            ]
    arrived = flat_ref[...]
    square_mean = jnp.sum(arrived * arrived, axis=1, keepdims=True) / width
    normed = (
        arrived * lax.rsqrt(square_mean + epsilon) * gain_ref[...].astype(jnp.float32)
    ).astype(jnp.bfloat16)
    gate_act = nt_dot(normed, gate_ref[...])
    up_act = nt_dot(normed, up_ref[...])
    hidden = (jax.nn.silu(gate_act) * up_act).astype(jnp.bfloat16)
    expert_out = jnp.dot(hidden, down_ref[...], preferred_element_type=jnp.float32)
    weighted = (expert_out * weight_ref[...]).astype(jnp.bfloat16)
    for tile in range(tiles):
        for plane in range(PLANES):
            at = plane * span + tile * 128
            fold_ref[tile * CAP : (tile + 1) * CAP, plane * 128 : (plane + 1) * 128] = weighted[
                :, at : at + 128
            ]
    back = jnp.dot(fold_ref[...], swap, preferred_element_type=jnp.float32).astype(jnp.bfloat16)
    for block in range(PLANE):
        tile, lane = block // 4, block % 4
        send_ref[block] = back[tile * CAP : (tile + 1) * CAP, lane * 128 : (lane + 1) * 128]


def expert_layer(inbound, norm_gain, weight, swap, gate_proj, up_proj, down_proj):
    width = norm_gain.shape[0]
    vmem = pl.BlockSpec(memory_space=pltpu.VMEM)
    return pl.pallas_call(
        expert_kernel,
        out_shape=jax.ShapeDtypeStruct(inbound.shape, jnp.bfloat16),
        in_specs=[vmem] * 7,
        out_specs=vmem,
        scratch_shapes=[
            pltpu.VMEM((PLANE // 4 * CAP, 512), jnp.bfloat16),
            pltpu.VMEM((CAP, width), jnp.float32),
        ],
        name="expert_layer",
    )(inbound, norm_gain.reshape(1, -1), weight, swap, gate_proj, up_proj, down_proj)


def combine_kernel(returned_ref, table_ref, parts_ref):
    column, cols, rows = parts_ref.shape
    returned = returned_ref[...].reshape(PLANE * CAP, PLANES * cols)
    moe = lax.dot_general(
        returned, table_ref[...], (((0,), (0,)), ((), ())), preferred_element_type=jnp.float32
    ).astype(jnp.bfloat16)
    for at in range(column):
        plane = at % PLANES
        parts_ref[at] = moe[plane * cols : (plane + 1) * cols]


def combine(returned, table, column, cols, rows):
    vmem = pl.BlockSpec(memory_space=pltpu.VMEM)
    return pl.pallas_call(
        combine_kernel,
        out_shape=jax.ShapeDtypeStruct((column, cols, rows), jnp.bfloat16),
        in_specs=[vmem] * 2,
        out_specs=vmem,
        name="combine",
    )(returned, table)


def shards(
    queries,
    cache_keys,
    cache_values,
    lengths,
    out_proj,
    residual,
    norm_gain,
    expert_ids,
    gate_weights,
    owners,
    gate_proj,
    up_proj,
    down_proj,
):
    rows, cols = residual.shape
    groups = lax.axis_size("sec")
    devices = lax.axis_size("dev")
    chips = devices // 2
    me = lax.axis_index("dev")
    table, weight, swap = routing(expert_ids, gate_weights, owners, me)

    head_out = attend(queries, cache_keys, cache_values, lengths)
    same_core = [[2 * chip + core for chip in range(chips)] for core in range(2)]
    swap_core = [(device, device ^ 1) for device in range(devices)]
    gathered = lax.all_to_all(
        jnp.broadcast_to(head_out[None], (chips,) + head_out.shape),
        "dev",
        0,
        0,
        tiled=True,
        axis_index_groups=same_core,
    )
    gathered = gathered.reshape(-1, head_out.shape[1])
    other = lax.ppermute(gathered, "dev", swap_core)
    own_part = nt_dot(out_proj, gathered).astype(jnp.bfloat16)
    other_part = nt_dot(out_proj, other).astype(jnp.bfloat16)
    first = me % 2 == 0
    part = jnp.concatenate(
        [jnp.where(first, own_part, other_part), jnp.where(first, other_part, own_part)], axis=1
    )
    share = cols // groups
    mine = lax.dynamic_slice_in_dim(residual.T, lax.axis_index("sec") * share, share, 0)
    block = jnp.concatenate([part, mine], axis=0)
    column = groups * PLANES
    columns = [
        [group * devices + plane * PLANE + at for group in range(groups) for plane in range(PLANES)]
        for at in range(PLANE)
    ]
    planes = [[plane * PLANE + at for at in range(PLANE)] for plane in range(PLANES)]
    block, table, weight, swap = lax.optimization_barrier((block, table, weight, swap))
    parts = lax.all_to_all(
        jnp.broadcast_to(block[None], (column,) + block.shape),
        ("sec", "dev"),
        0,
        0,
        tiled=True,
        axis_index_groups=columns,
    )
    outbound, base = dispatch(parts, table, me, cols)
    inbound = lax.all_to_all(outbound, "dev", 0, 0, tiled=True, axis_index_groups=planes)
    weighted = expert_layer(
        inbound, norm_gain, weight, swap, gate_proj[0], up_proj[0], down_proj[0]
    )
    returned = lax.all_to_all(weighted, "dev", 0, 0, tiled=True, axis_index_groups=planes)
    moe_parts = lax.all_to_all(
        combine(returned, table, column, cols, rows),
        ("sec", "dev"),
        0,
        0,
        tiled=True,
        axis_index_groups=columns,
    )
    moe = jnp.sum(moe_parts.astype(jnp.float32), axis=0)
    return (base + moe).astype(jnp.bfloat16).T


def solution(mesh):
    in_specs = (
        P("dev", "sec"),
        P("dev", "sec", None, None),
        P("dev", "sec", None, None),
        P("dev"),
        P("dev", "sec"),
        P(None, "dev"),
        P(),
        P(),
        P(),
        P(),
        P("dev", "sec", None),
        P("dev", "sec", None),
        P("dev", "sec", None),
    )
    out_specs = P(None, "dev")
    return jax.shard_map(shards, mesh=mesh, in_specs=in_specs, out_specs=out_specs, check_vma=False)
```

```python
import functools
import math

import jax
import jax.numpy as jnp
from jax import lax
from jax.experimental import pallas as pl
from jax.experimental.pallas import tpu as pltpu
from jax.sharding import PartitionSpec as P

epsilon = 1e-05

HALF = 64
BANDS = 2
PART = 24
ROW = 32


def attend(queries, cache_keys, cache_values, lengths):
    rows, kv_heads, key_span, head_dim = cache_keys.shape
    group_size = queries.shape[1] // (kv_heads * head_dim)
    grouped = queries.reshape(rows, kv_heads, group_size, head_dim)
    scores = jnp.einsum(
        "rkgd,rktd->rkgt", grouped, cache_keys, preferred_element_type=jnp.float32
    ) / math.sqrt(head_dim)
    live_mask = (
        jnp.arange(key_span, dtype=jnp.int32)[None, None, None, :] < lengths[:, None, None, None]
    )
    scores = jnp.where(live_mask, scores, -jnp.inf)
    row_top = jnp.max(scores, axis=-1, keepdims=True)
    raised = jnp.exp(scores - row_top)
    soft_weight = (raised / jnp.sum(raised, axis=-1, keepdims=True)).astype(jnp.bfloat16)
    head_out = jnp.einsum(
        "rkgt,rktd->rkgd", soft_weight, cache_values, preferred_element_type=jnp.float32
    )
    return head_out.astype(jnp.bfloat16).reshape(rows, -1)


def nt_dot(left, right):
    return lax.dot_general(
        left, right, (((1,), (1,)), ((), ())), preferred_element_type=jnp.float32
    )


def iota(shape, dim):
    return lax.broadcasted_iota(jnp.int32, shape, dim)


def one_hot(condition):
    return jnp.where(condition, 1.0, 0.0).astype(jnp.bfloat16)


def routing_kernel(me_ref, ids_ref, gates_ref, owners_ref, table_ref, weight_ref, swap_ref, slot_ref):
    top_count, rows = ids_ref.shape
    experts = owners_ref.shape[1]
    me = me_ref[0]
    ids = ids_ref[...]
    owners = owners_ref[...]
    named = jnp.zeros((experts, rows), jnp.float32)
    expert_at = iota((experts, rows), 0)
    for k in range(top_count):
        named = jnp.where(ids[k : k + 1, :] == expert_at, 1.0, named)
    holds = one_hot(owners == iota((HALF, experts), 0) + me // HALF * HALF)
    routed = jnp.dot(holds, named.astype(jnp.bfloat16), preferred_element_type=jnp.float32)
    earlier = one_hot(iota((rows, rows), 0) < iota((rows, rows), 1))
    before = jnp.dot(routed.astype(jnp.bfloat16), earlier, preferred_element_type=jnp.float32)
    slots = jnp.where(routed > 0.5, before, -1.0)
    slot_ref[...] = slots

    mine = jnp.sum(
        jnp.where(owners == me, iota(owners.shape, 1), 0), axis=1, keepdims=True
    )
    row_gate = jnp.sum(jnp.where(ids == mine, gates_ref[...], 0.0), axis=0, keepdims=True)
    row_slot = jnp.sum(
        jnp.where(iota(slots.shape, 0) == me % HALF, slots, 0.0), axis=0, keepdims=True
    )
    at = iota((BANDS * ROW, rows), 0)
    place = jnp.where(at % ROW < PART, at // ROW * PART + at % ROW, 4 * rows).astype(jnp.float32)
    weight_ref[...] = jnp.sum(jnp.where(row_slot == place, row_gate, 0.0), axis=1, keepdims=True)

    lanes = swap_ref.shape[0]
    source = iota((lanes, lanes), 0)
    target = iota((lanes, lanes), 1)
    swapped = target % 32 + target // 128 * 32 + target // 32 % 4 * 128
    swap_ref[...] = one_hot(source == swapped)

    for holder in range(HALF):
        for band in range(BANDS):
            table_ref[holder * ROW : (holder + 1) * ROW, band * rows : (band + 1) * rows] = one_hot(
                slot_ref[holder : holder + 1, :] == place[band * ROW : (band + 1) * ROW]
            )


def routing(expert_ids, gate_weights, owners, me):
    rows, top_count = expert_ids.shape
    vmem = pl.BlockSpec(memory_space=pltpu.VMEM)
    return pl.pallas_call(
        routing_kernel,
        out_shape=(
            jax.ShapeDtypeStruct((HALF * ROW, BANDS * rows), jnp.bfloat16),
            jax.ShapeDtypeStruct((BANDS * ROW, 1), jnp.float32),
            jax.ShapeDtypeStruct((512, 512), jnp.bfloat16),
        ),
        in_specs=[pl.BlockSpec(memory_space=pltpu.SMEM), vmem, vmem, vmem],
        out_specs=(vmem, vmem, vmem),
        scratch_shapes=[pltpu.VMEM((HALF, rows), jnp.float32)],
        name="routing",
    )(me.reshape(1), expert_ids.T, gate_weights.T, owners.reshape(1, -1))


def project_kernel(me_ref, heads_ref, own_ref, other_ref, residual_ref, parts_ref, part_ref, *, groups):
    own = own_ref.shape[0]
    span = heads_ref.shape[0]
    width = own_ref.shape[1]
    half = me_ref[0] // HALF
    heads = heads_ref[...]
    scale = 1.0 / groups
    start = pl.multiple_of(half * span, span)
    mine = nt_dot(own_ref[...], heads)
    mine = mine + residual_ref[:, pl.ds(start, span)].astype(jnp.float32) * scale
    theirs = nt_dot(other_ref[:, :width], heads)
    theirs = theirs + other_ref[:, width:].astype(jnp.float32) * scale
    part_ref[pl.ds(pl.multiple_of(half * own, own), own), :] = mine
    part_ref[pl.ds(pl.multiple_of((1 - half) * own, own), own), :] = theirs
    part = part_ref[...].astype(jnp.bfloat16)
    for at in range(parts_ref.shape[0]):
        parts_ref[at] = part


def project(heads, own, other, residual, me, groups):
    span = heads.shape[0]
    cols = own.shape[0]
    vmem = pl.BlockSpec(memory_space=pltpu.VMEM)
    return pl.pallas_call(
        functools.partial(project_kernel, groups=groups),
        out_shape=jax.ShapeDtypeStruct((groups * 2, 2 * cols, span), jnp.bfloat16),
        in_specs=[pl.BlockSpec(memory_space=pltpu.SMEM)] + [vmem] * 4,
        out_specs=vmem,
        scratch_shapes=[pltpu.VMEM((2 * cols, span), jnp.float32)],
        name="project",
    )(me.reshape(1), heads, own, other, residual)


def dispatch_kernel(me_ref, parts_ref, table_ref, send_ref, base_ref, sum_ref, wide_ref):
    column, cols, span = parts_ref.shape
    rows = 2 * span
    own = base_ref.shape[0]
    for half in range(2):
        total = parts_ref[half].astype(jnp.float32)
        for group in range(1, column // 2):
            total = total + parts_ref[group * 2 + half].astype(jnp.float32)
        sum_ref[:, half * span : (half + 1) * span] = total
    base_ref[...] = sum_ref[pl.ds(pl.multiple_of(me_ref[0] // HALF * own, own), own), :]
    hidden_in = sum_ref[...].astype(jnp.bfloat16)
    wide_ref[...] = jnp.zeros(wide_ref.shape, jnp.bfloat16)
    for band in range(BANDS):
        wide_ref[band * cols : (band + 1) * cols, band * rows : (band + 1) * rows] = hidden_in
    sent = nt_dot(table_ref[...], wide_ref[...]).astype(jnp.bfloat16)
    send_ref[...] = sent.reshape(HALF, ROW, BANDS * cols)[:, :PART, :]


def dispatch(parts, table, me):
    cols = parts.shape[1]
    rows = 2 * parts.shape[2]
    vmem = pl.BlockSpec(memory_space=pltpu.VMEM)
    return pl.pallas_call(
        dispatch_kernel,
        out_shape=(
            jax.ShapeDtypeStruct((HALF, PART, BANDS * cols), jnp.bfloat16),
            jax.ShapeDtypeStruct((cols // 2, rows), jnp.float32),
        ),
        in_specs=[pl.BlockSpec(memory_space=pltpu.SMEM), vmem, vmem],
        out_specs=(vmem, vmem),
        scratch_shapes=[
            pltpu.VMEM((cols, rows), jnp.float32),
            pltpu.VMEM((BANDS * cols, BANDS * rows), jnp.bfloat16),
        ],
        name="dispatch",
    )(me.reshape(1), parts, table)


def expert_kernel(
    inbound_ref, gain_ref, weight_ref, swap_ref, gate_ref, up_ref, down_ref, send_ref, fold_ref, flat_ref
):
    width = gain_ref.shape[1]
    pieces = []
    for tile in range(HALF // 4):
        for band in range(BANDS):
            for high in range(2):
                at = (tile // 8 + 2 * high) * (width // 4) + tile % 8 * 128
                pieces.append((tile * ROW, band * 2 + high, band * ROW, at))
    fold_ref[...] = jnp.zeros(fold_ref.shape, fold_ref.dtype)
    for block in range(HALF):
        tile, lane = block // 4, block % 4
        fold_ref[tile * ROW : tile * ROW + PART, lane * 128 : (lane + 1) * 128] = inbound_ref[block]
    swap = swap_ref[...]
    turned = jnp.dot(fold_ref[...], swap, preferred_element_type=jnp.float32)
    for row, lane, place, at in pieces:
        flat_ref[place : place + ROW, at : at + 128] = turned[
            row : row + ROW, lane * 128 : (lane + 1) * 128
        ]
    arrived = flat_ref[...]
    square_mean = jnp.sum(arrived * arrived, axis=1, keepdims=True) / width
    normed = (
        arrived * lax.rsqrt(square_mean + epsilon) * gain_ref[...].astype(jnp.float32)
    ).astype(jnp.bfloat16)
    gate_act = nt_dot(normed, gate_ref[...])
    up_act = nt_dot(normed, up_ref[...])
    hidden = (jax.nn.silu(gate_act) * up_act).astype(jnp.bfloat16)
    expert_out = jnp.dot(hidden, down_ref[...], preferred_element_type=jnp.float32)
    weighted = (expert_out * weight_ref[...]).astype(jnp.bfloat16)
    for row, lane, place, at in pieces:
        fold_ref[row : row + ROW, lane * 128 : (lane + 1) * 128] = weighted[
            place : place + ROW, at : at + 128
        ]
    back = jnp.dot(fold_ref[...], swap, preferred_element_type=jnp.float32).astype(jnp.bfloat16)
    for block in range(HALF):
        tile, lane = block // 4, block % 4
        send_ref[block] = back[tile * ROW : tile * ROW + PART, lane * 128 : (lane + 1) * 128]


def expert_layer(inbound, norm_gain, weight, swap, gate_proj, up_proj, down_proj):
    width = norm_gain.shape[0]
    vmem = pl.BlockSpec(memory_space=pltpu.VMEM)
    return pl.pallas_call(
        expert_kernel,
        out_shape=jax.ShapeDtypeStruct(inbound.shape, jnp.bfloat16),
        in_specs=[vmem] * 7,
        out_specs=vmem,
        scratch_shapes=[
            pltpu.VMEM((HALF // 4 * ROW, 512), jnp.bfloat16),
            pltpu.VMEM((BANDS * ROW, width), jnp.float32),
        ],
        name="expert_layer",
    )(inbound, norm_gain.reshape(1, -1), weight, swap, gate_proj, up_proj, down_proj)


def combine_kernel(returned_ref, table_ref, parts_ref, rows_ref):
    column, own, rows = parts_ref.shape
    cols = 2 * own
    rows_ref[...] = jnp.zeros(rows_ref.shape, rows_ref.dtype)
    for block in range(HALF):
        rows_ref[block * ROW : block * ROW + PART, :] = returned_ref[block]
    mixed = lax.dot_general(
        rows_ref[...], table_ref[...], (((0,), (0,)), ((), ())), preferred_element_type=jnp.float32
    )
    moe = (mixed[:cols, :rows] + mixed[cols:, rows:]).astype(jnp.bfloat16)
    for at in range(column):
        parts_ref[at] = moe[at % 2 * own : (at % 2 + 1) * own]


def combine(returned, table, column, own, rows):
    vmem = pl.BlockSpec(memory_space=pltpu.VMEM)
    return pl.pallas_call(
        combine_kernel,
        out_shape=jax.ShapeDtypeStruct((column, own, rows), jnp.bfloat16),
        in_specs=[vmem] * 2,
        out_specs=vmem,
        scratch_shapes=[pltpu.VMEM((HALF * ROW, 2 * BANDS * own), jnp.bfloat16)],
        name="combine",
    )(returned, table)


def shards(
    queries,
    cache_keys,
    cache_values,
    lengths,
    out_proj,
    residual,
    norm_gain,
    expert_ids,
    gate_weights,
    owners,
    gate_proj,
    up_proj,
    down_proj,
):
    rows, cols = residual.shape
    groups = lax.axis_size("sec")
    devices = lax.axis_size("dev")
    column = groups * 2
    me = lax.axis_index("dev")
    halves = [[half * HALF + at for at in range(HALF)] for half in range(2)]
    columns = [
        [group * devices + half * HALF + at for group in range(groups) for half in range(2)]
        for at in range(HALF)
    ]

    def over(x, axis, groups_of):
        return lax.all_to_all(x, axis, 0, 0, tiled=True, axis_index_groups=groups_of)

    facing = [(device, device ^ HALF) for device in range(devices)]
    residual = residual.T
    half_rows = rows // 2
    wanted = lax.dynamic_slice_in_dim(residual, (1 - me // HALF) * half_rows, half_rows, 1)
    other = lax.ppermute(jnp.concatenate([out_proj, wanted], axis=1), "dev", facing)

    head_out = attend(queries, cache_keys, cache_values, lengths)
    head_out, expert_ids = lax.optimization_barrier((head_out, expert_ids))
    table, weight, swap = routing(expert_ids, gate_weights, owners, me)
    heads = over(jnp.broadcast_to(head_out[None], (HALF,) + head_out.shape), "dev", halves)
    parts = project(heads.reshape(half_rows, -1), out_proj, other, residual, me, groups)
    parts, table, weight, swap = lax.optimization_barrier((parts, table, weight, swap))
    parts = over(parts, ("sec", "dev"), columns)
    outbound, base = dispatch(parts, table, me)
    inbound = over(outbound, "dev", halves)
    weighted = expert_layer(
        inbound, norm_gain, weight, swap, gate_proj[0], up_proj[0], down_proj[0]
    )
    returned = over(weighted, "dev", halves)
    moe_parts = over(combine(returned, table, column, cols, rows), ("sec", "dev"), columns)
    moe = jnp.sum(moe_parts.astype(jnp.float32), axis=0)
    return (base + moe).astype(jnp.bfloat16).T


def solution(mesh):
    in_specs = (
        P("dev", "sec"),
        P("dev", "sec", None, None),
        P("dev", "sec", None, None),
        P("dev"),
        P("dev", "sec"),
        P(None, "dev"),
        P(),
        P(),
        P(),
        P(),
        P("dev", "sec", None),
        P("dev", "sec", None),
        P("dev", "sec", None),
    )
    out_specs = P(None, "dev")
    return jax.shard_map(shards, mesh=mesh, in_specs=in_specs, out_specs=out_specs, check_vma=False)
```

```python
import functools
import math

import jax
import jax.numpy as jnp
from jax import lax
from jax.experimental import pallas as pl
from jax.experimental.pallas import tpu as pltpu
from jax.sharding import PartitionSpec as P

epsilon = 1e-05

HALF = 64
BANDS = 2
PART = 24
ROW = 32
VMEM_LIMIT = 24 << 20


def nt_dot(left, right):
    return lax.dot_general(
        left, right, (((1,), (1,)), ((), ())), preferred_element_type=jnp.float32
    )


def iota(shape, dim):
    return lax.broadcasted_iota(jnp.int32, shape, dim)


def near(*arrays):
    return tuple(pltpu.with_memory_space_constraint(array, pltpu.VMEM) for array in arrays)


def far(*arrays):
    return tuple(pltpu.with_memory_space_constraint(array, pltpu.HBM) for array in arrays)


def one_hot(condition):
    return jnp.where(condition, 1.0, 0.0).astype(jnp.bfloat16)


def attend_kernel(
    lengths_ref,
    queries_hbm,
    keys_hbm,
    values_hbm,
    out_ref,
    query_ref,
    queries_ref,
    keys_ref,
    values_ref,
    sems,
):
    copies = [
        pltpu.make_async_copy(source, target, sems.at[at])
        for at, (source, target) in enumerate(
            ((queries_hbm, queries_ref), (keys_hbm, keys_ref), (values_hbm, values_ref))
        )
    ]
    for copy in copies:
        copy.start()
    rows, _, key_span, head_dim = keys_ref.shape
    group_size = queries_ref.shape[1] // head_dim
    position = iota((group_size, key_span), 1)
    copies[0].wait()
    queries = queries_ref[...].astype(jnp.float32)
    outs = []
    copies[1].wait()
    for row in range(rows):
        for head in range(group_size):
            query_ref[row, head : head + 1, :] = queries[
                row : row + 1, head * head_dim : (head + 1) * head_dim
            ]
        scores = nt_dot(query_ref[row].astype(jnp.bfloat16), keys_ref[row, 0]) / math.sqrt(head_dim)
        scores = jnp.where(position < lengths_ref[row], scores, -jnp.inf)
        row_top = jnp.max(scores, axis=-1, keepdims=True)
        raised = jnp.exp(scores - row_top)
        soft_weight = (raised / jnp.sum(raised, axis=-1, keepdims=True)).astype(jnp.bfloat16)
        if row == 0:
            copies[2].wait()
        outs.append(jnp.dot(soft_weight, values_ref[row, 0], preferred_element_type=jnp.float32))
    for head in range(group_size):
        pair = jnp.concatenate([out[head : head + 1, :] for out in outs], axis=0)
        out_ref[:, head * head_dim : (head + 1) * head_dim] = pair.astype(jnp.bfloat16)


def attend(queries, cache_keys, cache_values, lengths):
    rows, width = queries.shape
    head_dim = cache_keys.shape[3]
    vmem = pl.BlockSpec(memory_space=pltpu.VMEM)
    return pl.pallas_call(
        attend_kernel,
        out_shape=pltpu.VMEM(queries.shape, jnp.bfloat16),
        in_specs=[pl.BlockSpec(memory_space=pltpu.SMEM)]
        + [pl.BlockSpec(memory_space=pltpu.HBM)] * 3,
        out_specs=vmem,
        scratch_shapes=[
            pltpu.VMEM((rows, width // head_dim, head_dim), jnp.float32),
            pltpu.VMEM(queries.shape, jnp.bfloat16),
            pltpu.VMEM(cache_keys.shape, jnp.bfloat16),
            pltpu.VMEM(cache_values.shape, jnp.bfloat16),
            pltpu.SemaphoreType.DMA((3,)),
        ],
        name="attend",
        compiler_params=pltpu.CompilerParams(vmem_limit_bytes=VMEM_LIMIT),
    )(*far(lengths, queries, cache_keys, cache_values))


def routing_kernel(me_ref, ids_ref, gates_ref, owners_ref, table_ref, weight_ref, swap_ref, slot_ref):
    top_count, rows = ids_ref.shape
    experts = owners_ref.shape[1]
    me = me_ref[0]
    ids = ids_ref[...]
    owners = owners_ref[...]
    named = jnp.zeros((experts, rows), jnp.float32)
    expert_at = iota((experts, rows), 0)
    for k in range(top_count):
        named = jnp.where(ids[k : k + 1, :] == expert_at, 1.0, named)
    holds = one_hot(owners == iota((HALF, experts), 0) + me // HALF * HALF)
    routed = jnp.dot(holds, named.astype(jnp.bfloat16), preferred_element_type=jnp.float32)
    earlier = one_hot(iota((rows, rows), 0) < iota((rows, rows), 1))
    before = jnp.dot(routed.astype(jnp.bfloat16), earlier, preferred_element_type=jnp.float32)
    slots = jnp.where(routed > 0.5, before, -1.0)
    slot_ref[...] = slots

    mine = jnp.sum(
        jnp.where(owners == me, iota(owners.shape, 1), 0), axis=1, keepdims=True
    )
    row_gate = jnp.sum(jnp.where(ids == mine, gates_ref[...], 0.0), axis=0, keepdims=True)
    row_slot = jnp.sum(
        jnp.where(iota(slots.shape, 0) == me % HALF, slots, 0.0), axis=0, keepdims=True
    )
    at = iota((BANDS * ROW, rows), 0)
    place = jnp.where(at % ROW < PART, at // ROW * PART + at % ROW, 4 * rows).astype(jnp.float32)
    weight_ref[...] = jnp.sum(jnp.where(row_slot == place, row_gate, 0.0), axis=1, keepdims=True)

    lanes = swap_ref.shape[0]
    source = iota((lanes, lanes), 0)
    target = iota((lanes, lanes), 1)
    swapped = target % 32 + target // 128 * 32 + target // 32 % 4 * 128
    swap_ref[...] = one_hot(source == swapped)

    for holder in range(HALF):
        for band in range(BANDS):
            table_ref[holder * ROW : (holder + 1) * ROW, band * rows : (band + 1) * rows] = one_hot(
                slot_ref[holder : holder + 1, :] == place[band * ROW : (band + 1) * ROW]
            )


def routing(expert_ids, gate_weights, owners, me):
    rows, top_count = expert_ids.shape
    vmem = pl.BlockSpec(memory_space=pltpu.VMEM)
    return pl.pallas_call(
        routing_kernel,
        out_shape=(
            pltpu.VMEM((HALF * ROW, BANDS * rows), jnp.bfloat16),
            pltpu.VMEM((BANDS * ROW, 1), jnp.float32),
            pltpu.VMEM((512, 512), jnp.bfloat16),
        ),
        in_specs=[pl.BlockSpec(memory_space=pltpu.SMEM), vmem, vmem, vmem],
        out_specs=(vmem, vmem, vmem),
        scratch_shapes=[pltpu.VMEM((HALF, rows), jnp.float32)],
        name="routing",
        compiler_params=pltpu.CompilerParams(vmem_limit_bytes=VMEM_LIMIT),
    )(me.reshape(1), *near(expert_ids.T, gate_weights.T, owners.reshape(1, -1)))


def project_kernel(me_ref, heads_ref, own_ref, other_ref, residual_ref, parts_ref, part_ref, *, groups):
    own = own_ref.shape[0]
    span = heads_ref.shape[0]
    width = own_ref.shape[1]
    half = me_ref[0] // HALF
    heads = heads_ref[...]
    scale = 1.0 / groups
    start = pl.multiple_of(half * span, span)
    mine = nt_dot(own_ref[...], heads)
    mine = mine + residual_ref[:, pl.ds(start, span)].astype(jnp.float32) * scale
    theirs = nt_dot(other_ref[:, :width], heads)
    theirs = theirs + other_ref[:, width:].astype(jnp.float32) * scale
    part_ref[pl.ds(pl.multiple_of(half * own, own), own), :] = mine
    part_ref[pl.ds(pl.multiple_of((1 - half) * own, own), own), :] = theirs
    part = part_ref[...].astype(jnp.bfloat16)
    for at in range(parts_ref.shape[0]):
        parts_ref[at] = part


def project(heads, own, other, residual, me, groups):
    span = heads.shape[0]
    cols = own.shape[0]
    vmem = pl.BlockSpec(memory_space=pltpu.VMEM)
    return pl.pallas_call(
        functools.partial(project_kernel, groups=groups),
        out_shape=pltpu.VMEM((groups * 2, 2 * cols, span), jnp.bfloat16),
        in_specs=[pl.BlockSpec(memory_space=pltpu.SMEM)] + [vmem] * 4,
        out_specs=vmem,
        scratch_shapes=[pltpu.VMEM((2 * cols, span), jnp.float32)],
        name="project",
        compiler_params=pltpu.CompilerParams(vmem_limit_bytes=VMEM_LIMIT),
    )(me.reshape(1), *near(heads, own, other, residual))


def dispatch_kernel(me_ref, parts_ref, table_ref, send_ref, base_ref, sum_ref, wide_ref):
    column, cols, span = parts_ref.shape
    rows = 2 * span
    own = base_ref.shape[0]
    for half in range(2):
        total = parts_ref[half].astype(jnp.float32)
        for group in range(1, column // 2):
            total = total + parts_ref[group * 2 + half].astype(jnp.float32)
        sum_ref[:, half * span : (half + 1) * span] = total
    base_ref[...] = sum_ref[pl.ds(pl.multiple_of(me_ref[0] // HALF * own, own), own), :]
    hidden_in = sum_ref[...].astype(jnp.bfloat16)
    wide_ref[...] = jnp.zeros(wide_ref.shape, jnp.bfloat16)
    for band in range(BANDS):
        wide_ref[band * cols : (band + 1) * cols, band * rows : (band + 1) * rows] = hidden_in
    sent = nt_dot(table_ref[...], wide_ref[...]).astype(jnp.bfloat16)
    send_ref[...] = sent.reshape(HALF, ROW, BANDS * cols)[:, :PART, :]


def dispatch(parts, table, me):
    cols = parts.shape[1]
    rows = 2 * parts.shape[2]
    vmem = pl.BlockSpec(memory_space=pltpu.VMEM)
    return pl.pallas_call(
        dispatch_kernel,
        out_shape=(
            pltpu.VMEM((HALF, PART, BANDS * cols), jnp.bfloat16),
            pltpu.VMEM((cols // 2, rows), jnp.float32),
        ),
        in_specs=[pl.BlockSpec(memory_space=pltpu.SMEM), vmem, vmem],
        out_specs=(vmem, vmem),
        scratch_shapes=[
            pltpu.VMEM((cols, rows), jnp.float32),
            pltpu.VMEM((BANDS * cols, BANDS * rows), jnp.bfloat16),
        ],
        name="dispatch",
        compiler_params=pltpu.CompilerParams(vmem_limit_bytes=VMEM_LIMIT),
    )(me.reshape(1), *near(parts, table))


def expert_kernel(
    inbound_ref,
    gain_ref,
    weight_ref,
    swap_ref,
    gate_hbm,
    up_hbm,
    down_hbm,
    send_ref,
    fold_ref,
    flat_ref,
    gate_ref,
    up_ref,
    down_ref,
    sems,
):
    copies = [
        pltpu.make_async_copy(source, target, sems.at[at])
        for at, (source, target) in enumerate(
            ((gate_hbm, gate_ref), (up_hbm, up_ref), (down_hbm, down_ref))
        )
    ]
    for copy in copies:
        copy.start()
    width = gain_ref.shape[1]
    pieces = []
    for tile in range(HALF // 4):
        for band in range(BANDS):
            for high in range(2):
                at = (tile // 8 + 2 * high) * (width // 4) + tile % 8 * 128
                pieces.append((tile * ROW, band * 2 + high, band * ROW, at))
    fold_ref[...] = jnp.zeros(fold_ref.shape, fold_ref.dtype)
    for block in range(HALF):
        tile, lane = block // 4, block % 4
        fold_ref[tile * ROW : tile * ROW + PART, lane * 128 : (lane + 1) * 128] = inbound_ref[block]
    swap = swap_ref[...]
    turned = jnp.dot(fold_ref[...], swap, preferred_element_type=jnp.float32)
    for row, lane, place, at in pieces:
        flat_ref[place : place + ROW, at : at + 128] = turned[
            row : row + ROW, lane * 128 : (lane + 1) * 128
        ]
    arrived = flat_ref[...]
    square_mean = jnp.sum(arrived * arrived, axis=1, keepdims=True) / width
    normed = (
        arrived * lax.rsqrt(square_mean + epsilon) * gain_ref[...].astype(jnp.float32)
    ).astype(jnp.bfloat16)
    copies[0].wait()
    gate_act = nt_dot(normed, gate_ref[...])
    copies[1].wait()
    up_act = nt_dot(normed, up_ref[...])
    hidden = (jax.nn.silu(gate_act) * up_act).astype(jnp.bfloat16)
    copies[2].wait()
    expert_out = jnp.dot(hidden, down_ref[...], preferred_element_type=jnp.float32)
    weighted = (expert_out * weight_ref[...]).astype(jnp.bfloat16)
    for row, lane, place, at in pieces:
        fold_ref[row : row + ROW, lane * 128 : (lane + 1) * 128] = weighted[
            place : place + ROW, at : at + 128
        ]
    back = jnp.dot(fold_ref[...], swap, preferred_element_type=jnp.float32).astype(jnp.bfloat16)
    for block in range(HALF):
        tile, lane = block // 4, block % 4
        send_ref[block] = back[tile * ROW : tile * ROW + PART, lane * 128 : (lane + 1) * 128]


def expert_layer(inbound, norm_gain, weight, swap, gate_proj, up_proj, down_proj):
    width = norm_gain.shape[1]
    vmem = pl.BlockSpec(memory_space=pltpu.VMEM)
    return pl.pallas_call(
        expert_kernel,
        out_shape=pltpu.VMEM(inbound.shape, jnp.bfloat16),
        in_specs=[vmem] * 4 + [pl.BlockSpec(memory_space=pltpu.HBM)] * 3,
        out_specs=vmem,
        scratch_shapes=[
            pltpu.VMEM((HALF // 4 * ROW, 512), jnp.bfloat16),
            pltpu.VMEM((BANDS * ROW, width), jnp.float32),
            pltpu.VMEM(gate_proj.shape, jnp.bfloat16),
            pltpu.VMEM(up_proj.shape, jnp.bfloat16),
            pltpu.VMEM(down_proj.shape, jnp.bfloat16),
            pltpu.SemaphoreType.DMA((3,)),
        ],
        name="expert_layer",
        compiler_params=pltpu.CompilerParams(vmem_limit_bytes=VMEM_LIMIT),
    )(*near(inbound, norm_gain, weight, swap), *far(gate_proj, up_proj, down_proj))


def combine_kernel(returned_ref, table_ref, parts_ref, rows_ref):
    column, own, rows = parts_ref.shape
    cols = 2 * own
    rows_ref[...] = jnp.zeros(rows_ref.shape, rows_ref.dtype)
    for block in range(HALF):
        rows_ref[block * ROW : block * ROW + PART, :] = returned_ref[block]
    mixed = lax.dot_general(
        rows_ref[...], table_ref[...], (((0,), (0,)), ((), ())), preferred_element_type=jnp.float32
    )
    moe = (mixed[:cols, :rows] + mixed[cols:, rows:]).astype(jnp.bfloat16)
    for at in range(column):
        parts_ref[at] = moe[at % 2 * own : (at % 2 + 1) * own]


def combine(returned, table, column, own, rows):
    vmem = pl.BlockSpec(memory_space=pltpu.VMEM)
    return pl.pallas_call(
        combine_kernel,
        out_shape=pltpu.VMEM((column, own, rows), jnp.bfloat16),
        in_specs=[vmem] * 2,
        out_specs=vmem,
        scratch_shapes=[pltpu.VMEM((HALF * ROW, 2 * BANDS * own), jnp.bfloat16)],
        name="combine",
        compiler_params=pltpu.CompilerParams(vmem_limit_bytes=VMEM_LIMIT),
    )(*near(returned, table))


def shards(
    queries,
    cache_keys,
    cache_values,
    lengths,
    out_proj,
    residual,
    norm_gain,
    expert_ids,
    gate_weights,
    owners,
    gate_proj,
    up_proj,
    down_proj,
):
    rows, cols = residual.shape
    groups = lax.axis_size("sec")
    devices = lax.axis_size("dev")
    column = groups * 2
    me = lax.axis_index("dev")
    halves = [[half * HALF + at for at in range(HALF)] for half in range(2)]
    columns = [
        [group * devices + half * HALF + at for group in range(groups) for half in range(2)]
        for at in range(HALF)
    ]

    def over(x, axis, groups_of):
        return lax.all_to_all(x, axis, 0, 0, tiled=True, axis_index_groups=groups_of)

    facing = [(device, device ^ HALF) for device in range(devices)]
    residual = residual.T
    half_rows = rows // 2
    wanted = lax.dynamic_slice_in_dim(residual, (1 - me // HALF) * half_rows, half_rows, 1)
    other = lax.ppermute(jnp.concatenate([out_proj, wanted], axis=1), "dev", facing)

    head_out = attend(queries, cache_keys, cache_values, lengths)
    head_out, expert_ids = lax.optimization_barrier((head_out, expert_ids))
    table, weight, swap = routing(expert_ids, gate_weights, owners, me)
    heads = over(jnp.broadcast_to(head_out[None], (HALF,) + head_out.shape), "dev", halves)
    parts = project(heads.reshape(half_rows, -1), out_proj, other, residual, me, groups)
    gain = norm_gain.reshape(1, -1)
    parts, table, weight, swap, gain = lax.optimization_barrier(
        (parts, table, weight, swap, gain)
    )
    parts = over(parts, ("sec", "dev"), columns)
    outbound, base = dispatch(parts, table, me)
    inbound = over(outbound, "dev", halves)
    weighted = expert_layer(
        inbound, gain, weight, swap, gate_proj[0], up_proj[0], down_proj[0]
    )
    returned = over(weighted, "dev", halves)
    moe_parts = over(combine(returned, table, column, cols, rows), ("sec", "dev"), columns)
    moe = jnp.sum(moe_parts.astype(jnp.float32), axis=0)
    return (base + moe).astype(jnp.bfloat16).T


def solution(mesh):
    in_specs = (
        P("dev", "sec"),
        P("dev", "sec", None, None),
        P("dev", "sec", None, None),
        P("dev"),
        P("dev", "sec"),
        P(None, "dev"),
        P(),
        P(),
        P(),
        P(),
        P("dev", "sec", None),
        P("dev", "sec", None),
        P("dev", "sec", None),
    )
    out_specs = P(None, "dev")
    return jax.shard_map(shards, mesh=mesh, in_specs=in_specs, out_specs=out_specs, check_vma=False)
```
